256 devices in a mesh: pair: 8 (over x_lo, y), outv: 8 (over z), conv: 4 (over x_hi, core).
Axes of the slice: x: 4 (x_hi: 2, x_lo: 2; x = x_hi * 2 + x_lo), y: 4, z: 8, core: 2. Of those that a mesh axis runs over, the one named last changes fastest.
Arguments:
- amplitudes: bfloat16 [16384, 6144], P('pair', ('conv', 'outv')), may hold values from -6 to 6
- integrals: bfloat16 [6144, 12288], P('conv', ('outv', 'pair')), may hold values from -0.21875 to 0.21875
- amp_mask: int32 [8, 64], P('pair', 'conv'), may hold values from 0 to 1, as said below
- int_mask: int32 [64, 128], P('conv', 'outv'), may hold values 0 or 1
Outputs:
- ladder: bfloat16 [12288, 16384], P(('outv', 'conv'), 'pair')
The draws below stay inside these ranges and needn't reach their ends.
Inputs may be any that keep to these rules, and one draw needn't show every extreme that they name: `amp_mask`: 0 or 1; the share of ones differs from pair tile to pair tile.
All inputs are finite; a program needn't handle non-finite values. No bound on the sum of `int_mask` on one device may be relied on, other than what follows from the above.
Results may differ from the reference program's by a relative error of at most 0.001.
Values may be sent and summed in bfloat16 or wider, within the bound.
No kernel may reach another device: no remote copies, remote signals or barrier semaphores. Data moves between devices by JAX's collectives and lax.ppermute only.
A program may use at most 64 MiB of HBM per device.

```python
import jax
import jax.numpy as jnp
from jax import lax

TW = 96
PTILE = 2048
PTILES = 8
PAIRS = 16384
KT = 64
NT = 128


def draw_amp_mask(key, part):
    level = jax.random.randint(jax.random.fold_in(key, 11), (PTILES, 1), 2, 9)
    pick = jax.random.randint(jax.random.fold_in(key, 12), (PTILES, KT), 0, 8)
    return (pick < level).astype(jnp.int32)


def with_ends(array, stream_key, smallest, top_value):
    longest = array.shape.index(max(array.shape))
    spots = []
    for shift in (0, 1):
        where = [jax.random.randint(jax.random.fold_in(stream_key, axis), (), 0, length) for axis, length in enumerate(array.shape)]
        where[longest] = (where[longest] + shift) % array.shape[longest]
        spots.append(tuple(where))
    return array.at[spots[0]].set(smallest).at[spots[1]].set(top_value)


def spiked(entries, stream_key, source, target, parts, factor):
    def block_of(position):
        return (jnp.arange(entries.shape[position]) // (entries.shape[position] // parts)).reshape((-1,) + (1,) * (entries.ndim - 1 - position))

    near = jax.random.permutation(stream_key, parts)[block_of(target)]
    other_side = (block_of(target) + parts // 2) % parts
    return jnp.where((block_of(source) == near) | (block_of(source) == other_side), factor * entries, entries)


def steps_of(stream_key, dims, shards, low, top_value):
    loudness = 1.0
    for dim, shards_of in shards:
        draws = jax.random.uniform(jax.random.fold_in(jax.random.fold_in(stream_key, 6), dim), (shards_of,), jnp.float32, low / len(shards), top_value / len(shards))
        loudness = loudness * jnp.repeat(jnp.exp(draws), dims[dim] // shards_of).reshape((-1,) + (1,) * (len(dims) - 1 - dim))
    return loudness


def scatter_about(own_key, shape, scale, reach, pieces=(), dtype=jnp.bfloat16):
    result = jax.random.normal(own_key, shape, jnp.float32) * scale
    if len(pieces) > 0:
        result = steps_of(own_key, shape, pieces, -0.22, 0.18) * result
    return jnp.clip(result, min=-reach, max=reach).astype(dtype)


def bell_draw_with(key, dims, spread, limit, shards, heavy, held_as=jnp.bfloat16):
    entries = spread * jax.random.normal(key, dims, jnp.float32)
    if shards:
        entries = entries * steps_of(key, dims, shards, -0.22, 0.18)
    return jnp.clip(spiked(entries, jax.random.fold_in(key, 3), *heavy), -limit, limit).astype(held_as)


def setup_inputs(seed: int = 0) -> dict:
    keys = jax.random.split(jax.random.key(seed), 5)
    return {
        "amplitudes": scatter_about(keys[0], (PAIRS, KT * TW), 1.0, 6.0, ((0, 8), (1, 32))),
        "integrals": bell_draw_with(keys[1], (KT * TW, NT * TW), (KT * TW) ** -0.5, 0.21875, ((0, 4), (1, 64)), (0, 1, 64, 4.0)),
        "amp_mask": draw_amp_mask(jax.random.fold_in(keys[4], 71), 0),
        "int_mask": with_ends((jax.random.randint(keys[3], (KT, NT), 0, 4) < 3).astype(jnp.int32), jax.random.fold_in(keys[3], 1), 0, 1),
    }


def reference(amplitudes, integrals, amp_mask, int_mask):
    amp_blocks = (amplitudes.reshape(PTILES, PTILE, KT, TW) * amp_mask[:, None, :, None].astype(jnp.bfloat16)).reshape(PAIRS, KT * TW)
    int_blocks = (integrals.reshape(KT, TW, NT, TW) * int_mask[:, None, :, None].astype(jnp.bfloat16)).reshape(KT * TW, NT * TW)
    ladder = lax.dot_general(int_blocks, amp_blocks, (((0,), (1,)), ((), ())), preferred_element_type=jnp.float32)
    return ladder.astype(jnp.bfloat16)
```

```python
import jax
import jax.numpy as jnp
from jax import lax
from jax.experimental import pallas as pl
from jax.experimental.pallas import tpu as pltpu
from jax.sharding import PartitionSpec as P

TW = 96
AXES = ("pair", "outv", "conv")
NX, NY, NZ = 4, 4, 8
RCHUNKS = 2
VMEM = pltpu.MemorySpace.VMEM
SMEM = pltpu.MemorySpace.SMEM


def index_of(x, y, z, c):
    x, y, z = x % NX, y % NY, z % NZ
    return ((x % 2) * NY + y) * (NZ * 4) + z * 4 + (x // 2) * 2 + c


def moves(target):
    return [
        (index_of(x, y, z, c), index_of(*target(x, y, z, c)))
        for x in range(NX)
        for y in range(NY)
        for z in range(NZ)
        for c in range(2)
    ]


def sign(i, c):
    return 1 - 2 * ((i + c) % 2)


X_FIRST = moves(lambda x, y, z, c: (x + sign(x, c), y, z, c))
X_OTHER = moves(lambda x, y, z, c: (x - sign(x, c), y, z, c))
Y_FIRST = moves(lambda x, y, z, c: (x, y + sign(y, c), z, c))
Y_OTHER = moves(lambda x, y, z, c: (x, y - sign(y, c), z, c))
Z_FIRST = moves(lambda x, y, z, c: (x, y, z + sign(z, c), c))
Z_OTHER = moves(lambda x, y, z, c: (x, y, z - sign(z, c), c))
X_ACROSS = moves(lambda x, y, z, c: (x + 2, y, z, c))
CORE = moves(lambda x, y, z, c: (x, y, z, 1 - c))
RING4 = (0, 1, -1, -2)
RING8 = (0, 1, -1, -2, 2, 3, -3, -4)


def send(array, plan):
    return lax.ppermute(array, AXES, plan)


def mask_integrals_kernel(place, mask_ref, int_ref, first_ref, second_ref):
    width = int_ref.shape[1]
    half = width // 2
    tile = lax.broadcasted_iota(jnp.int32, (8, width), 1) // TW
    for j in range(int_ref.shape[0] // TW):
        column = place[0] * (int_ref.shape[0] // TW) + j
        row = jnp.zeros((8, width), jnp.float32)
        for k in range(width // TW):
            row = jnp.where(tile == k, mask_ref[k, column].astype(jnp.float32), row)
        row = row[0:1, :].astype(jnp.bfloat16)
        rows = pl.ds(j * TW, TW)
        first_ref[rows, :] = int_ref[rows, :half] * row[:, :half]
        second_ref[rows, :] = int_ref[rows, half:] * row[:, half:]


def mask_integrals(place, int_mask, int_t):
    rows, width = int_t.shape
    shape = jax.ShapeDtypeStruct((rows, width // 2), jnp.bfloat16)
    return pl.pallas_call(
        mask_integrals_kernel,
        in_specs=[pl.BlockSpec(memory_space=SMEM), pl.BlockSpec(memory_space=SMEM), pl.BlockSpec(memory_space=VMEM)],
        out_specs=[pl.BlockSpec(memory_space=VMEM)] * 2,
        out_shape=[shape, shape],
        name="mask_integrals",
    )(place, int_mask, int_t)


def mask_amplitudes_kernel(place, mask_ref, amp_ref, keep_ref, give_ref):
    half = amp_ref.shape[1] // 2
    for j in range(amp_ref.shape[0] // TW):
        value = mask_ref[0, place[1] * (amp_ref.shape[0] // TW) + j].astype(jnp.float32)
        rows = pl.ds(j * TW, TW)
        row = jnp.full((1, half), value, jnp.float32).astype(jnp.bfloat16)
        keep_ref[rows, :] = amp_ref[rows, pl.ds(pl.multiple_of(place[2] * half, 128), half)] * row
        give_ref[rows, :] = amp_ref[rows, pl.ds(pl.multiple_of((1 - place[2]) * half, 128), half)] * row


def mask_amplitudes(place, amp_mask, amp_t):
    rows, width = amp_t.shape
    shape = jax.ShapeDtypeStruct((rows, width // 2), jnp.bfloat16)
    return pl.pallas_call(
        mask_amplitudes_kernel,
        in_specs=[pl.BlockSpec(memory_space=SMEM), pl.BlockSpec(memory_space=SMEM), pl.BlockSpec(memory_space=VMEM)],
        out_specs=[pl.BlockSpec(memory_space=VMEM)] * 2,
        out_shape=[shape, shape],
        name="mask_amplitudes",
    )(place, amp_mask, amp_t)


def ring_of_eight(own):
    got = send(own, Z_FIRST)
    near = jnp.stack([own, got])
    second = send(near, Z_OTHER)
    third = send(second, Z_FIRST)
    fourth = send(third, Z_OTHER)
    return [near, second, third, fourth]


def plane(own, first_axis, second_axis):
    got = send(own, first_axis[0])
    near = jnp.stack([own, got])
    far = send(near, first_axis[1])
    pieces = []
    for group in (near, far):
        step = send(group, second_axis[0])
        pieces += [group, step, send(group, second_axis[1]), send(step, second_axis[1])]
    return pieces


def multiply_kernel(own, rchunk, place, *refs):
    n_int, n_amp = 16, 8
    int_refs, amp_refs = refs[:n_int], refs[n_int : n_int + n_amp]
    rest = list(refs[n_int + n_amp :])
    other_ref = rest.pop(0) if own else None
    outs = [rest.pop(0) for _ in range(2 if own else 1)]
    int_v, amp_v, int_sems, amp_sems = rest
    x, y, z, c = place[3], place[4], place[1], place[5]
    x_hi = place[2]
    core = c if own else 1 - c
    sx, sy, sz = 1 - 2 * ((x + c) % 2), 1 - 2 * ((y + c) % 2), 1 - 2 * ((z + c) % 2)
    rows, depth, width = 192, 768, amp_v.shape[1]

    amp_copies = []
    for chain in range(2):
        hi = x_hi if chain == 0 else 1 - x_hi
        for step in range(4):
            for e in range(2):
                z_from = (z + sz * RING8[2 * step + e] + 8) % 8
                row = pl.multiple_of((hi * 8 + z_from) * rows, rows)
                amp_copies.append(
                    pltpu.make_async_copy(
                        amp_refs[chain * 4 + step].at[e, :, pl.ds(rchunk * width, width)],
                        amp_v.at[pl.ds(row, rows), :],
                        amp_sems.at[len(amp_copies)],
                    )
                )
    int_copies = []
    for half in range(2):
        for group in range(2):
            for step in range(4):
                for e in range(2):
                    near, far = RING4[2 * group + e], RING4[step]
                    dx, dy = (near, far) if half == 0 else (far, near)
                    x_from, y_from = (x + sx * dx + 4) % 4, (y + sy * dy + 4) % 4
                    block = ((x_from % 2 + x_hi + 1) % 2) * 2 + y_from % 2
                    row = pl.multiple_of(block * rows, rows)
                    col = pl.multiple_of((x_from // 2) * 2 * depth + half * depth, 128)
                    copy = pltpu.make_async_copy(
                        int_refs[half * 8 + group * 4 + step].at[e],
                        int_v.at[pl.ds(row, rows), pl.ds(col, depth)],
                        int_sems.at[len(int_copies)],
                    )
                    int_copies.append((y_from // 2 == core, copy))
    for copy in amp_copies:
        copy.start()
    for here, copy in int_copies:
        pl.when(here)(copy.start)
    for copy in amp_copies:
        copy.wait()
    for here, copy in int_copies:
        pl.when(here)(copy.wait)

    size = 128
    for part in range(2):
        @pl.loop(0, 384 // size)
        def _(i):
            src = pl.ds(pl.multiple_of(part * 384 + i * size, size), size)
            total = jnp.dot(int_v[src, :], amp_v[...], preferred_element_type=jnp.float32)
            if own:
                dst = pl.ds(pl.multiple_of(i * size, size), size)
                outs[part][dst, :] = (total + other_ref[src, :]).astype(jnp.bfloat16)
            else:
                outs[0][src, :] = total


def multiply(own, rchunk, place, ints, amps, other=None):
    width = 1024 // RCHUNKS
    if own:
        shapes = [jax.ShapeDtypeStruct((384, width), jnp.bfloat16)] * 2
    else:
        shapes = [jax.ShapeDtypeStruct((768, width), jnp.float32)]
    any_spec = pl.BlockSpec(memory_space=pl.ANY)
    specs = [pl.BlockSpec(memory_space=SMEM)] + [any_spec] * (len(ints) + len(amps))
    args = [place, *ints, *amps]
    if own:
        specs.append(pl.BlockSpec(memory_space=VMEM))
        args.append(other)

    def kernel(*refs):
        multiply_kernel(own, rchunk, *refs)

    out = pl.pallas_call(
        kernel,
        in_specs=specs,
        out_specs=[pl.BlockSpec(memory_space=VMEM)] * len(shapes),
        out_shape=shapes,
        scratch_shapes=[
            pltpu.VMEM((768, 3072), jnp.bfloat16),
            pltpu.VMEM((3072, width), jnp.bfloat16),
            pltpu.SemaphoreType.DMA((32,)),
            pltpu.SemaphoreType.DMA((16,)),
        ],
        compiler_params=pltpu.CompilerParams(vmem_limit_bytes=40 * 1024 * 1024),
        cost_estimate=pl.CostEstimate(
            flops=2 * 768 * 3072 * width, bytes_accessed=768 * 3072 * 2 + 3072 * width * 2 + 768 * width * 4, transcendentals=0
        ),
        name="multiply_own" if own else "multiply_other",
    )(*args)
    return out


def body(amplitudes, integrals, amp_mask, int_mask):
    pair, z, conv = (lax.axis_index(name) for name in AXES)
    x_hi, core = conv // 2, conv % 2
    x_lo, y = pair // NY, pair % NY
    place = jnp.stack([pair, z, x_hi, x_hi * 2 + x_lo, y, core]).astype(jnp.int32)

    first, second = mask_integrals(place, int_mask, integrals.T)
    keep, give = mask_amplitudes(place, amp_mask, amplitudes.T)
    partner = send(give, X_ACROSS)
    amps = ring_of_eight(keep) + ring_of_eight(partner)
    ints = plane(first, (X_FIRST, X_OTHER), (Y_FIRST, Y_OTHER)) + plane(second, (Y_FIRST, Y_OTHER), (X_FIRST, X_OTHER))

    kept, received = [], []
    for r in range(RCHUNKS):
        (partial,) = multiply(False, r, place, ints, amps)
        other = send(partial, CORE)
        theirs, mine = multiply(True, r, place, ints, amps, other)
        kept.append(mine)
        received.append(send(theirs, X_ACROSS))
    low = [jnp.where(x_hi == 0, k, g) for k, g in zip(kept, received)]
    high = [jnp.where(x_hi == 0, g, k) for k, g in zip(kept, received)]
    return jnp.concatenate(low + high, axis=1)


def solution(mesh):
    placed = (
        P("pair", ("conv", "outv")),
        P("conv", ("outv", "pair")),
        P("pair", "conv"),
        P("conv", "outv"),
    )
    return jax.shard_map(
        body, mesh=mesh, in_specs=placed, out_specs=P(("outv", "conv"), "pair"), check_vma=False
    )
```

```python
import jax
import jax.numpy as jnp
from jax import lax
from jax.experimental import pallas as pl
from jax.experimental.pallas import tpu as pltpu
from jax.sharding import PartitionSpec as P

TW = 96
AXES = ("pair", "outv", "conv")
NX, NY, NZ = 4, 4, 8
RCHUNKS = 2
MIB = 1024 * 1024
VMEM = pltpu.MemorySpace.VMEM
SMEM = pltpu.MemorySpace.SMEM


def index_of(x, y, z, c):
    x, y, z = x % NX, y % NY, z % NZ
    return ((x % 2) * NY + y) * (NZ * 4) + z * 4 + (x // 2) * 2 + c


def moves(target):
    return [
        (index_of(x, y, z, c), index_of(*target(x, y, z, c)))
        for x in range(NX)
        for y in range(NY)
        for z in range(NZ)
        for c in range(2)
    ]


def sign(i, c):
    return 1 - 2 * ((i + c) % 2)


X_FIRST = moves(lambda x, y, z, c: (x + sign(x, c), y, z, c))
X_OTHER = moves(lambda x, y, z, c: (x - sign(x, c), y, z, c))
Y_FIRST = moves(lambda x, y, z, c: (x, y + sign(y, c), z, c))
Y_OTHER = moves(lambda x, y, z, c: (x, y - sign(y, c), z, c))
Z_FIRST = moves(lambda x, y, z, c: (x, y, z + sign(z, c), c))
Z_OTHER = moves(lambda x, y, z, c: (x, y, z - sign(z, c), c))
X_ACROSS = moves(lambda x, y, z, c: (x + 2, y, z, c))
CORE = moves(lambda x, y, z, c: (x, y, z, 1 - c))
RING4 = (0, 1, -1, -2)
RING8 = (0, 1, -1, -2, 2, 3, -3, -4)


def send(array, plan):
    return lax.ppermute(array, AXES, plan)


def mask_integrals_kernel(place, mask_ref, int_ref, first_ref, second_ref):
    width = int_ref.shape[1]
    half = width // 2
    tile = lax.broadcasted_iota(jnp.int32, (8, width), 1) // TW
    for j in range(int_ref.shape[0] // TW):
        column = place[0] * (int_ref.shape[0] // TW) + j
        row = jnp.zeros((8, width), jnp.float32)
        for k in range(width // TW):
            row = jnp.where(tile == k, mask_ref[k, column].astype(jnp.float32), row)
        row = row[0:1, :].astype(jnp.bfloat16)
        rows = pl.ds(j * TW, TW)
        first_ref[rows, :] = int_ref[rows, :half] * row[:, :half]
        second_ref[rows, :] = int_ref[rows, half:] * row[:, half:]


def mask_integrals(place, int_mask, int_t):
    rows, width = int_t.shape
    shape = jax.ShapeDtypeStruct((rows, width // 2), jnp.bfloat16)
    return pl.pallas_call(
        mask_integrals_kernel,
        in_specs=[pl.BlockSpec(memory_space=SMEM), pl.BlockSpec(memory_space=SMEM), pl.BlockSpec(memory_space=VMEM)],
        out_specs=[pl.BlockSpec(memory_space=VMEM)] * 2,
        out_shape=[shape, shape],
        compiler_params=pltpu.CompilerParams(vmem_limit_bytes=8 * MIB),
        name="mask_integrals",
    )(place, int_mask, int_t)


def mask_amplitudes_kernel(place, mask_ref, amp_ref, keep_ref, give_ref):
    width = keep_ref.shape[2]
    for j in range(amp_ref.shape[0] // TW):
        value = mask_ref[0, place[1] * (amp_ref.shape[0] // TW) + j].astype(jnp.float32)
        rows = pl.ds(j * TW, TW)
        row = jnp.full((1, width), value, jnp.float32).astype(jnp.bfloat16)
        for out_ref, side in ((keep_ref, place[2]), (give_ref, 1 - place[2])):
            for r in range(RCHUNKS):
                first = (side * RCHUNKS + r) * width
                out_ref[r, rows, :] = amp_ref[rows, pl.ds(pl.multiple_of(first, 128), width)] * row


def mask_amplitudes(place, amp_mask, amp_t):
    rows, width = amp_t.shape
    shape = jax.ShapeDtypeStruct((RCHUNKS, rows, width // (2 * RCHUNKS)), jnp.bfloat16)
    return pl.pallas_call(
        mask_amplitudes_kernel,
        in_specs=[pl.BlockSpec(memory_space=SMEM), pl.BlockSpec(memory_space=SMEM), pl.BlockSpec(memory_space=VMEM)],
        out_specs=[pl.BlockSpec(memory_space=VMEM)] * 2,
        out_shape=[shape] * 2,
        compiler_params=pltpu.CompilerParams(vmem_limit_bytes=8 * MIB),
        name="mask_amplitudes",
    )(place, amp_mask, amp_t)


def ring_of_eight(near):
    second = send(near, Z_OTHER)
    third = send(second, Z_FIRST)
    fourth = send(third, Z_OTHER)
    return [near, second, third, fourth]


def plane(own, first_axis, second_axis):
    near = jnp.stack([own, send(own, first_axis[0])])
    far = send(near, first_axis[1])
    pieces = []
    for group in (near, far):
        both = jnp.concatenate([group, send(group, second_axis[0])])
        pieces += [both, send(both, second_axis[1])]
    return pieces


def order_amplitudes_kernel(first_step, steps, place, *refs):
    pieces = refs[:steps]
    out_ref, sems = refs[-2:]
    z, x_hi, c = place[1], place[2], place[5]
    rows = pieces[0].shape[1]
    sz = 1 - 2 * ((z + c) % 2)
    copies = []
    for step, piece in enumerate(pieces):
        for chain in range(2):
            hi = x_hi if chain == 0 else 1 - x_hi
            for e in range(2):
                z_from = (z + sz * RING8[2 * (first_step + step) + e] + NZ) % NZ
                row = pl.multiple_of((hi * NZ + z_from) * rows, rows)
                copies.append(
                    pltpu.make_async_copy(
                        piece.at[2 * chain + e], out_ref.at[pl.ds(row, rows), :], sems.at[len(copies)]
                    )
                )
    for copy in copies:
        copy.start()
    for copy in copies:
        copy.wait()


def order_amplitudes(place, pieces):
    _, rows, width = pieces[0].shape
    any_spec, vmem_spec = pl.BlockSpec(memory_space=pl.ANY), pl.BlockSpec(memory_space=VMEM)
    out = pltpu.VMEM((16 * rows, width), jnp.bfloat16)
    held = None
    for first, steps in ((0, 3), (3, 1)):
        args = [place, *pieces[first : first + steps]] + ([] if held is None else [held])

        def kernel(*refs, first=first, steps=steps):
            order_amplitudes_kernel(first, steps, *refs)

        held = pl.pallas_call(
            kernel,
            in_specs=[pl.BlockSpec(memory_space=SMEM)] + [any_spec] * steps + [vmem_spec] * (held is not None),
            out_specs=vmem_spec,
            out_shape=out,
            scratch_shapes=[pltpu.SemaphoreType.DMA((4 * steps,))],
            input_output_aliases={} if held is None else {len(args) - 1: 0},
            cost_estimate=pl.CostEstimate(flops=0, bytes_accessed=16 * steps * rows * width, transcendentals=0),
            compiler_params=pltpu.CompilerParams(vmem_limit_bytes=MIB),
            name="order_amplitudes",
        )(*args)
    return held


def order_integrals_kernel(got, place, *refs):
    pieces = refs[:4]
    outs, sems = refs[-3:-1], refs[-1]
    x, y, c, x_hi = place[3], place[4], place[5], place[2]
    sx, sy = 1 - 2 * ((x + c) % 2), 1 - 2 * ((y + c) % 2)
    rows, depth = pieces[0].shape[1:]
    copies = []
    for half in range(2):
        for group in range(2):
            for step in range(2):
                for e in range(2):
                    near, far = RING4[2 * group + e], RING4[2 * got + step]
                    dx, dy = (near, far) if half == 0 else (far, near)
                    x_from, y_from = (x + sx * dx + NX) % NX, (y + sy * dy + NY) % NY
                    side = (x_from % 2 + x_hi + 1) % 2
                    row = pl.multiple_of((side * 2 + y_from % 2) * rows, rows)
                    col = pl.multiple_of((x_from // 2) * 2 * depth + half * depth, 128)
                    for own in range(2):
                        copy = pltpu.make_async_copy(
                            pieces[half * 2 + group].at[step * 2 + e],
                            outs[own].at[pl.ds(row, rows), pl.ds(col, depth)],
                            sems.at[len(copies)],
                        )
                        copies.append((y_from // 2 == (c if own else 1 - c), copy))
    for here, copy in copies:
        pl.when(here)(copy.start)
    for here, copy in copies:
        pl.when(here)(copy.wait)


def order_integrals(place, ints):
    any_spec, vmem_spec = pl.BlockSpec(memory_space=pl.ANY), pl.BlockSpec(memory_space=VMEM)
    out = pltpu.VMEM((768, 3072), jnp.bfloat16)
    held = []
    for got in range(2):
        args = [place, *ints[got::2], *held]

        def kernel(*refs, got=got):
            order_integrals_kernel(got, *refs)

        held = pl.pallas_call(
            kernel,
            in_specs=[pl.BlockSpec(memory_space=SMEM)] + [any_spec] * 4 + [vmem_spec] * len(held),
            out_specs=[vmem_spec] * 2,
            out_shape=[out] * 2,
            scratch_shapes=[pltpu.SemaphoreType.DMA((32,))],
            input_output_aliases={5: 0, 6: 1} if held else {},
            cost_estimate=pl.CostEstimate(flops=0, bytes_accessed=2 * 768 * 3072 * 2, transcendentals=0),
            compiler_params=pltpu.CompilerParams(vmem_limit_bytes=MIB),
            name="order_integrals",
        )(*args)
    return held


def multiply_kernel(own, int_ref, amp_ref, *refs):
    rows = 384
    for part in range(2):
        src = pl.ds(part * rows, rows)
        total = jnp.dot(int_ref[src, :], amp_ref[...], preferred_element_type=jnp.float32)
        if own:
            other_ref, outs = refs[0], refs[1:]
            outs[part][...] = (total + other_ref[src, :]).astype(jnp.bfloat16)
        else:
            refs[0][src, :] = total


def multiply(own, ints, amps, other=None):
    width = amps.shape[1]
    if own:
        shapes = [jax.ShapeDtypeStruct((384, width), jnp.bfloat16)] * 2
    else:
        shapes = [jax.ShapeDtypeStruct((768, width), jnp.float32)]
    vmem_spec = pl.BlockSpec(memory_space=VMEM)
    args = [ints, amps] + ([other] if own else [])

    def kernel(*refs):
        multiply_kernel(own, *refs)

    return pl.pallas_call(
        kernel,
        in_specs=[vmem_spec] * len(args),
        out_specs=[vmem_spec] * len(shapes),
        out_shape=shapes,
        cost_estimate=pl.CostEstimate(
            flops=2 * 768 * 3072 * width, bytes_accessed=768 * 3072 * 2 + 3072 * width * 2 + 768 * width * 4, transcendentals=0
        ),
        compiler_params=pltpu.CompilerParams(vmem_limit_bytes=12 * MIB),
        name="multiply_own" if own else "multiply_other",
    )(*args)


def body(amplitudes, integrals, amp_mask, int_mask):
    pair, z, conv = (lax.axis_index(name) for name in AXES)
    x_hi, core = conv // 2, conv % 2
    x_lo, y = pair // NY, pair % NY
    place = jnp.stack([pair, z, x_hi, x_hi * 2 + x_lo, y, core]).astype(jnp.int32)

    first, second = mask_integrals(place, int_mask, integrals.T)
    place, first, second = lax.optimization_barrier((place, first, second))
    keep, give = mask_amplitudes(place, amp_mask, amplitudes.T)
    keep_got = send(keep, Z_FIRST)
    partner = send(give, X_ACROSS)
    partner_got = send(partner, Z_FIRST)
    ints = plane(first, (X_FIRST, X_OTHER), (Y_FIRST, Y_OTHER)) + plane(second, (Y_FIRST, Y_OTHER), (X_FIRST, X_OTHER))
    amps = [
        order_amplitudes(place, ring_of_eight(jnp.stack([keep[r], keep_got[r], partner[r], partner_got[r]])))
        for r in range(RCHUNKS)
    ]
    other_ints, own_ints = order_integrals(place, ints)

    kept, received = [], []
    for columns in amps:
        (partial,) = multiply(False, other_ints, columns)
        theirs, mine = multiply(True, own_ints, columns, send(partial, CORE))
        kept.append(mine)
        received.append(send(theirs, X_ACROSS))
    low = [jnp.where(x_hi == 0, k, g) for k, g in zip(kept, received)]
    high = [jnp.where(x_hi == 0, g, k) for k, g in zip(kept, received)]
    return jnp.concatenate(low + high, axis=1)


def solution(mesh):
    placed = (
        P("pair", ("conv", "outv")),
        P("conv", ("outv", "pair")),
        P("pair", "conv"),
        P("conv", "outv"),
    )
    return jax.shard_map(
        body, mesh=mesh, in_specs=placed, out_specs=P(("outv", "conv"), "pair"), check_vma=False
    )
```

```python
import jax
import jax.numpy as jnp
from jax import lax
from jax.experimental import pallas as pl
from jax.experimental.pallas import tpu as pltpu
from jax.sharding import PartitionSpec as P

TW = 96
AXES = ("pair", "outv", "conv")
NX, NY, NZ = 4, 4, 8
RCHUNKS = 2
DEPTH_X = 896
MIB = 1024 * 1024
VMEM = pltpu.MemorySpace.VMEM
SMEM = pltpu.MemorySpace.SMEM


def index_of(x, y, z, c):
    x, y, z = x % NX, y % NY, z % NZ
    return ((x % 2) * NY + y) * (NZ * 4) + z * 4 + (x // 2) * 2 + c


def moves(target):
    return [
        (index_of(x, y, z, c), index_of(*target(x, y, z, c)))
        for x in range(NX)
        for y in range(NY)
        for z in range(NZ)
        for c in range(2)
    ]


def sign(i, c):
    return 1 - 2 * ((i + c) % 2)


X_FIRST = moves(lambda x, y, z, c: (x + sign(x, c), y, z, c))
X_OTHER = moves(lambda x, y, z, c: (x - sign(x, c), y, z, c))
Y_FIRST = moves(lambda x, y, z, c: (x, y + sign(y, c), z, c))
Y_OTHER = moves(lambda x, y, z, c: (x, y - sign(y, c), z, c))
Z_FIRST = moves(lambda x, y, z, c: (x, y, z + sign(z, c), c))
Z_OTHER = moves(lambda x, y, z, c: (x, y, z - sign(z, c), c))
X_ACROSS = moves(lambda x, y, z, c: (x + 2, y, z, c))
CORE = moves(lambda x, y, z, c: (x, y, z, 1 - c))
RING4 = (0, 1, -1, -2)
RING8 = (0, 1, -1, -2, 2, 3, -3, -4)


def send(array, plan):
    return lax.ppermute(array, AXES, plan)


def mask_integrals_kernel(place, mask_ref, int_ref, first_ref, second_ref):
    width = int_ref.shape[1]
    half = first_ref.shape[1]
    tile = lax.broadcasted_iota(jnp.int32, (8, width), 1) // TW
    for j in range(int_ref.shape[0] // TW):
        column = place[0] * (int_ref.shape[0] // TW) + j
        row = jnp.zeros((8, width), jnp.float32)
        for k in range(width // TW):
            row = jnp.where(tile == k, mask_ref[k, column].astype(jnp.float32), row)
        row = row[0:1, :].astype(jnp.bfloat16)
        rows = pl.ds(j * TW, TW)
        first_ref[rows, :] = int_ref[rows, :half] * row[:, :half]
        second_ref[rows, :] = int_ref[rows, half:] * row[:, half:]


def mask_integrals(place, int_mask, int_t):
    rows, width = int_t.shape
    shapes = [jax.ShapeDtypeStruct((rows, depth), jnp.bfloat16) for depth in (DEPTH_X, width - DEPTH_X)]
    return pl.pallas_call(
        mask_integrals_kernel,
        in_specs=[pl.BlockSpec(memory_space=SMEM), pl.BlockSpec(memory_space=SMEM), pl.BlockSpec(memory_space=VMEM)],
        out_specs=[pl.BlockSpec(memory_space=VMEM)] * 2,
        out_shape=shapes,
        compiler_params=pltpu.CompilerParams(vmem_limit_bytes=8 * MIB),
        name="mask_integrals",
    )(place, int_mask, int_t)


def mask_amplitudes_kernel(place, mask_ref, amp_ref, keep_ref, give_ref):
    width = keep_ref.shape[2]
    for j in range(amp_ref.shape[0] // TW):
        value = mask_ref[0, place[1] * (amp_ref.shape[0] // TW) + j].astype(jnp.float32)
        rows = pl.ds(j * TW, TW)
        row = jnp.full((1, width), value, jnp.float32).astype(jnp.bfloat16)
        for out_ref, side in ((keep_ref, place[2]), (give_ref, 1 - place[2])):
            for r in range(RCHUNKS):
                first = (side * RCHUNKS + r) * width
                out_ref[r, rows, :] = amp_ref[rows, pl.ds(pl.multiple_of(first, 128), width)] * row


def mask_amplitudes(place, amp_mask, amp_t):
    rows, width = amp_t.shape
    shape = jax.ShapeDtypeStruct((RCHUNKS, rows, width // (2 * RCHUNKS)), jnp.bfloat16)
    return pl.pallas_call(
        mask_amplitudes_kernel,
        in_specs=[pl.BlockSpec(memory_space=SMEM), pl.BlockSpec(memory_space=SMEM), pl.BlockSpec(memory_space=VMEM)],
        out_specs=[pl.BlockSpec(memory_space=VMEM)] * 2,
        out_shape=[shape] * 2,
        compiler_params=pltpu.CompilerParams(vmem_limit_bytes=8 * MIB),
        name="mask_amplitudes",
    )(place, amp_mask, amp_t)


def after(array, *others):
    return lax.optimization_barrier((array, *others))[0]


def ring_of_eight(near):
    second = send(near, Z_OTHER)
    third = send(second, Z_FIRST)
    fourth = send(third, Z_OTHER)
    return [near, second, third, fourth]


def plane(own, first_axis, second_axis):
    near = jnp.stack([own, send(own, first_axis[0])])
    far = send(near, first_axis[1])
    pieces = []
    for group in (near, far):
        both = jnp.concatenate([group, send(group, second_axis[0])])
        pieces += [both, send(both, second_axis[1])]
    return pieces


def order_amplitudes_kernel(first_step, steps, place, *refs):
    pieces = refs[:steps]
    out_ref, sems = refs[-2:]
    z, x_hi, c = place[1], place[2], place[5]
    rows = pieces[0].shape[1]
    sz = 1 - 2 * ((z + c) % 2)
    copies = []
    for step, piece in enumerate(pieces):
        for chain in range(2):
            hi = x_hi if chain == 0 else 1 - x_hi
            for e in range(2):
                z_from = (z + sz * RING8[2 * (first_step + step) + e] + NZ) % NZ
                row = pl.multiple_of((hi * NZ + z_from) * rows, rows)
                for col in range(0, piece.shape[2], 128):
                    copies.append(
                        pltpu.make_async_copy(
                            piece.at[2 * chain + e, :, pl.ds(col, 128)],
                            out_ref.at[pl.ds(row, rows), pl.ds(col, 128)],
                            sems.at[len(copies)],
                        )
                    )
    for copy in copies:
        copy.start()
    for copy in copies:
        copy.wait()


def order_amplitudes(place, pieces, first_step, held=()):
    _, rows, width = pieces[0].shape
    steps = len(pieces)
    any_spec, vmem_spec = pl.BlockSpec(memory_space=pl.ANY), pl.BlockSpec(memory_space=VMEM)

    def kernel(*refs):
        order_amplitudes_kernel(first_step, steps, *refs)

    return pl.pallas_call(
        kernel,
        in_specs=[pl.BlockSpec(memory_space=SMEM)] + [any_spec] * steps + [vmem_spec] * len(held),
        out_specs=vmem_spec,
        out_shape=pltpu.VMEM((16 * rows, width), jnp.bfloat16),
        scratch_shapes=[pltpu.SemaphoreType.DMA((4 * steps * width // 128,))],
        input_output_aliases={1 + steps: 0} if held else {},
        cost_estimate=pl.CostEstimate(flops=0, bytes_accessed=16 * steps * rows * width, transcendentals=0),
        compiler_params=pltpu.CompilerParams(vmem_limit_bytes=MIB),
        name="order_amplitudes",
    )(place, *pieces, *held)


def order_integrals_kernel(got, place, *refs):
    pieces = refs[:4]
    outs, sems = refs[-3:-1], refs[-1]
    x, y, c, x_hi = place[3], place[4], place[5], place[2]
    sx, sy = 1 - 2 * ((x + c) % 2), 1 - 2 * ((y + c) % 2)
    rows, depths = pieces[0].shape[1], (pieces[0].shape[2], pieces[2].shape[2])
    copies = []
    for half in range(2):
        for group in range(2):
            for step in range(2):
                for e in range(2):
                    near, far = RING4[2 * group + e], RING4[2 * got + step]
                    dx, dy = (near, far) if half == 0 else (far, near)
                    x_from, y_from = (x + sx * dx + NX) % NX, (y + sy * dy + NY) % NY
                    side = (x_from % 2 + x_hi + 1) % 2
                    row = pl.multiple_of((side * 2 + y_from % 2) * rows, rows)
                    col = pl.multiple_of((x_from // 2) * sum(depths) + half * depths[0], 128)
                    for own in range(2):
                        copy = pltpu.make_async_copy(
                            pieces[half * 2 + group].at[step * 2 + e],
                            outs[own].at[pl.ds(row, rows), pl.ds(col, depths[half])],
                            sems.at[len(copies)],
                        )
                        copies.append((y_from // 2 == (c if own else 1 - c), copy))
    for here, copy in copies:
        pl.when(here)(copy.start)
    for here, copy in copies:
        pl.when(here)(copy.wait)


def order_integrals(place, ints):
    any_spec, vmem_spec = pl.BlockSpec(memory_space=pl.ANY), pl.BlockSpec(memory_space=VMEM)
    out = pltpu.VMEM((768, 3072), jnp.bfloat16)
    held = []
    for got in range(2):
        args = [place, *ints[got::2], *held]

        def kernel(*refs, got=got):
            order_integrals_kernel(got, *refs)

        held = pl.pallas_call(
            kernel,
            in_specs=[pl.BlockSpec(memory_space=SMEM)] + [any_spec] * 4 + [vmem_spec] * len(held),
            out_specs=[vmem_spec] * 2,
            out_shape=[out] * 2,
            scratch_shapes=[pltpu.SemaphoreType.DMA((32,))],
            input_output_aliases={5: 0, 6: 1} if held else {},
            cost_estimate=pl.CostEstimate(flops=0, bytes_accessed=2 * 768 * 3072 * 2, transcendentals=0),
            compiler_params=pltpu.CompilerParams(vmem_limit_bytes=MIB),
            name="order_integrals",
        )(*args)
    return held


def multiply_kernel(int_ref, amp_ref, *refs):
    rows = int_ref.shape[0] // 2
    other_refs, outs = refs[:-2], refs[-2:]
    for side in range(2):
        total = jnp.dot(int_ref[pl.ds(side * rows, rows), :], amp_ref[...], preferred_element_type=jnp.float32)
        if other_refs:
            total = (total + other_refs[side][...]).astype(jnp.bfloat16)
        outs[side][...] = total


def multiply(ints, amps, *other):
    rows, depth, width = ints.shape[0] // 2, ints.shape[1], amps.shape[1]
    vmem_spec = pl.BlockSpec(memory_space=VMEM)
    return pl.pallas_call(
        multiply_kernel,
        in_specs=[vmem_spec] * (2 + len(other)),
        out_specs=[vmem_spec] * 2,
        out_shape=[jax.ShapeDtypeStruct((rows, width), jnp.bfloat16 if other else jnp.float32)] * 2,
        cost_estimate=pl.CostEstimate(
            flops=4 * rows * depth * width, bytes_accessed=(2 * rows + width) * depth * 2 + 8 * rows * width, transcendentals=0
        ),
        compiler_params=pltpu.CompilerParams(vmem_limit_bytes=12 * MIB),
        name="multiply_own" if other else "multiply_other",
    )(ints, amps, *other)


def body(amplitudes, integrals, amp_mask, int_mask):
    pair, z, conv = (lax.axis_index(name) for name in AXES)
    x_hi, core = conv // 2, conv % 2
    x_lo, y = pair // NY, pair % NY
    place = jnp.stack([pair, z, x_hi, x_hi * 2 + x_lo, y, core]).astype(jnp.int32)

    first, second = mask_integrals(place, int_mask, integrals.T)
    place, first, second = lax.optimization_barrier((place, first, second))
    keep, give = mask_amplitudes(place, amp_mask, amplitudes.T)
    keep_got = send(keep, Z_FIRST)
    partner = send(give, X_ACROSS)
    partner_got = send(partner, Z_FIRST)
    ints = plane(first, (X_FIRST, X_OTHER), (Y_FIRST, Y_OTHER)) + plane(second, (Y_FIRST, Y_OTHER), (X_FIRST, X_OTHER))
    rings = [ring_of_eight(jnp.stack([keep[r], keep_got[r], partner[r], partner_got[r]])) for r in range(RCHUNKS)]
    held = [order_amplitudes(place, ring[:3], 0) for ring in rings]
    held[0] = after(*held)
    amps = [order_amplitudes(place, ring[3:], 3, [part]) for ring, part in zip(rings, held)]
    other_ints, own_ints = order_integrals(place, ints)

    kept, received = [], []
    for columns in amps:
        partials = [send(partial, CORE) for partial in multiply(other_ints, columns)]
        theirs, mine = multiply(own_ints, columns, *partials)
        kept.append(mine)
        received.append(send(theirs, X_ACROSS))
    low = [jnp.where(x_hi == 0, k, g) for k, g in zip(kept, received)]
    high = [jnp.where(x_hi == 0, g, k) for k, g in zip(kept, received)]
    return jnp.concatenate(low + high, axis=1)


def solution(mesh):
    placed = (
        P("pair", ("conv", "outv")),
        P("conv", ("outv", "pair")),
        P("pair", "conv"),
        P("conv", "outv"),
    )
    return jax.shard_map(
        body, mesh=mesh, in_specs=placed, out_specs=P(("outv", "conv"), "pair"), check_vma=False
    )
```

```python
import jax
import jax.numpy as jnp
from jax import lax
from jax.experimental import pallas as pl
from jax.experimental.pallas import tpu as pltpu
from jax.sharding import PartitionSpec as P

TW = 96
AXES = ("pair", "outv", "conv")
NX, NY, NZ = 4, 4, 8
RCHUNKS = 2
DEPTH_X = 768
MIB = 1024 * 1024
VMEM = pltpu.MemorySpace.VMEM
SMEM = pltpu.MemorySpace.SMEM


def index_of(x, y, z, c):
    x, y, z = x % NX, y % NY, z % NZ
    return ((x % 2) * NY + y) * (NZ * 4) + z * 4 + (x // 2) * 2 + c


def moves(target):
    return [
        (index_of(x, y, z, c), index_of(*target(x, y, z, c)))
        for x in range(NX)
        for y in range(NY)
        for z in range(NZ)
        for c in range(2)
    ]


def sign(i, c):
    return 1 - 2 * ((i + c) % 2)


X_FIRST = moves(lambda x, y, z, c: (x + sign(x, c), y, z, c))
X_OTHER = moves(lambda x, y, z, c: (x - sign(x, c), y, z, c))
Y_FIRST = moves(lambda x, y, z, c: (x, y + sign(y, c), z, c))
Y_OTHER = moves(lambda x, y, z, c: (x, y - sign(y, c), z, c))
Z_FIRST = moves(lambda x, y, z, c: (x, y, z + sign(z, c), c))
Z_OTHER = moves(lambda x, y, z, c: (x, y, z - sign(z, c), c))
X_ACROSS = moves(lambda x, y, z, c: (x + 2, y, z, c))
CORE = moves(lambda x, y, z, c: (x, y, z, 1 - c))
RING4 = (0, 1, -1, -2)
RING8 = (0, 1, -1, -2, 2, 3, -3, -4)


def send(array, plan):
    return lax.ppermute(array, AXES, plan)


def mask_integrals_kernel(place, mask_ref, int_ref, first_ref, second_ref):
    width = int_ref.shape[1]
    half = first_ref.shape[1]
    tile = lax.broadcasted_iota(jnp.int32, (8, width), 1) // TW
    for j in range(int_ref.shape[0] // TW):
        column = place[0] * (int_ref.shape[0] // TW) + j
        row = jnp.zeros((8, width), jnp.float32)
        for k in range(width // TW):
            row = jnp.where(tile == k, mask_ref[k, column].astype(jnp.float32), row)
        row = row[0:1, :].astype(jnp.bfloat16)
        rows = pl.ds(j * TW, TW)
        first_ref[rows, :] = int_ref[rows, :half] * row[:, :half]
        second_ref[rows, :] = int_ref[rows, half:] * row[:, half:]


def mask_integrals(place, int_mask, int_t):
    rows, width = int_t.shape
    shapes = [jax.ShapeDtypeStruct((rows, depth), jnp.bfloat16) for depth in (DEPTH_X, width - DEPTH_X)]
    return pl.pallas_call(
        mask_integrals_kernel,
        in_specs=[pl.BlockSpec(memory_space=SMEM), pl.BlockSpec(memory_space=SMEM), pl.BlockSpec(memory_space=VMEM)],
        out_specs=[pl.BlockSpec(memory_space=VMEM)] * 2,
        out_shape=shapes,
        compiler_params=pltpu.CompilerParams(vmem_limit_bytes=8 * MIB),
        name="mask_integrals",
    )(place, int_mask, int_t)


def mask_amplitudes_kernel(place, mask_ref, amp_ref, keep_ref, give_ref):
    width = keep_ref.shape[1]
    for j in range(amp_ref.shape[0] // TW):
        value = mask_ref[0, place[1] * (amp_ref.shape[0] // TW) + j].astype(jnp.float32)
        rows = pl.ds(j * TW, TW)
        row = jnp.full((1, width), value, jnp.float32).astype(jnp.bfloat16)
        for out_ref, side in ((give_ref, 1 - place[2]), (keep_ref, place[2])):
            out_ref[rows, :] = amp_ref[rows, pl.ds(pl.multiple_of(side * width, 128), width)] * row


def mask_amplitudes(place, amp_mask, amp_t):
    rows, width = amp_t.shape
    shape = jax.ShapeDtypeStruct((rows, width // 2), jnp.bfloat16)
    return pl.pallas_call(
        mask_amplitudes_kernel,
        in_specs=[pl.BlockSpec(memory_space=SMEM), pl.BlockSpec(memory_space=SMEM), pl.BlockSpec(memory_space=VMEM)],
        out_specs=[pl.BlockSpec(memory_space=VMEM)] * 2,
        out_shape=[shape] * 2,
        compiler_params=pltpu.CompilerParams(vmem_limit_bytes=8 * MIB),
        name="mask_amplitudes",
    )(place, amp_mask, amp_t)


def ring_of_eight(own):
    near = jnp.stack([own, send(own, Z_FIRST)])
    second = send(near, Z_OTHER)
    third = send(second, Z_FIRST)
    fourth = send(third, Z_OTHER)
    return [near, second, third, fourth]


def plane(own, first_axis, second_axis):
    near = jnp.stack([own, send(own, first_axis[0])])
    far = send(near, first_axis[1])
    pieces = []
    for group in (near, far):
        both = jnp.concatenate([group, send(group, second_axis[0])])
        pieces += [both, send(both, second_axis[1])]
    return pieces


def order_amplitudes_kernel(origins, place, *refs):
    pieces = refs[: len(origins)]
    out_ref, sems = refs[-2:]
    z, x_hi, c = place[1], place[2], place[5]
    rows = pieces[0].shape[1]
    sz = 1 - 2 * ((z + c) % 2)
    copies = []
    for (chain, step), piece in zip(origins, pieces):
        hi = x_hi if chain == 0 else 1 - x_hi
        for e in range(2):
            z_from = (z + sz * RING8[2 * step + e] + NZ) % NZ
            row = pl.multiple_of((hi * NZ + z_from) * rows, rows)
            for col in range(0, piece.shape[2], 256):
                copies.append(
                    pltpu.make_async_copy(
                        piece.at[e, :, pl.ds(col, 256)],
                        out_ref.at[pl.ds(row, rows), pl.ds(col, 256)],
                        sems.at[len(copies)],
                    )
                )
    for copy in copies:
        copy.start()
    for copy in copies:
        copy.wait()


def order_amplitudes(place, chains):
    _, rows, width = chains[0][0].shape
    any_spec, vmem_spec = pl.BlockSpec(memory_space=pl.ANY), pl.BlockSpec(memory_space=VMEM)
    held = []
    for origins in (((0, 0), (1, 0), (0, 1), (1, 1), (0, 2), (1, 2)), ((0, 3),), ((1, 3),)):
        pieces = [chains[chain][step] for chain, step in origins]

        def kernel(*refs, origins=origins):
            order_amplitudes_kernel(origins, *refs)

        held = [
            pl.pallas_call(
                kernel,
                in_specs=[pl.BlockSpec(memory_space=SMEM)] + [any_spec] * len(pieces) + [vmem_spec] * len(held),
                out_specs=vmem_spec,
                out_shape=pltpu.VMEM((16 * rows, width), jnp.bfloat16),
                scratch_shapes=[pltpu.SemaphoreType.DMA((2 * len(pieces) * width // 256,))],
                input_output_aliases={1 + len(pieces): 0} if held else {},
                cost_estimate=pl.CostEstimate(flops=0, bytes_accessed=8 * len(pieces) * rows * width, transcendentals=0),
                compiler_params=pltpu.CompilerParams(vmem_limit_bytes=MIB),
                name="order_amplitudes",
            )(place, *pieces, *held)
        ]
    return held[0]


def order_integrals_kernel(got, place, *refs):
    pieces = refs[:4]
    outs, sems = refs[-3:-1], refs[-1]
    x, y, c, x_hi = place[3], place[4], place[5], place[2]
    sx, sy = 1 - 2 * ((x + c) % 2), 1 - 2 * ((y + c) % 2)
    rows, depths = pieces[0].shape[1], (pieces[0].shape[2], pieces[2].shape[2])
    copies = []
    for half in range(2):
        for group in range(2):
            for step in range(2):
                for e in range(2):
                    near, far = RING4[2 * group + e], RING4[2 * got + step]
                    dx, dy = (near, far) if half == 0 else (far, near)
                    x_from, y_from = (x + sx * dx + NX) % NX, (y + sy * dy + NY) % NY
                    side = (x_from % 2 + x_hi + 1) % 2
                    row = pl.multiple_of((side * 2 + y_from % 2) * rows, rows)
                    col = pl.multiple_of((x_from // 2) * sum(depths) + half * depths[0], 128)
                    for own in range(2):
                        copy = pltpu.make_async_copy(
                            pieces[half * 2 + group].at[step * 2 + e],
                            outs[own].at[pl.ds(row, rows), pl.ds(col, depths[half])],
                            sems.at[len(copies)],
                        )
                        copies.append((y_from // 2 == (c if own else 1 - c), copy))
    for here, copy in copies:
        pl.when(here)(copy.start)
    for here, copy in copies:
        pl.when(here)(copy.wait)


def order_integrals(place, ints):
    any_spec, vmem_spec = pl.BlockSpec(memory_space=pl.ANY), pl.BlockSpec(memory_space=VMEM)
    out = pltpu.VMEM((768, 3072), jnp.bfloat16)
    held = []
    for got in range(2):
        args = [place, *ints[got::2], *held]

        def kernel(*refs, got=got):
            order_integrals_kernel(got, *refs)

        held = pl.pallas_call(
            kernel,
            in_specs=[pl.BlockSpec(memory_space=SMEM)] + [any_spec] * 4 + [vmem_spec] * len(held),
            out_specs=[vmem_spec] * 2,
            out_shape=[out] * 2,
            scratch_shapes=[pltpu.SemaphoreType.DMA((32,))],
            input_output_aliases={5: 0, 6: 1} if held else {},
            cost_estimate=pl.CostEstimate(flops=0, bytes_accessed=2 * 768 * 3072 * 2, transcendentals=0),
            compiler_params=pltpu.CompilerParams(vmem_limit_bytes=MIB),
            name="order_integrals",
        )(*args)
    return held


def multiply_kernel(cols, int_ref, amp_ref, *refs):
    rows = int_ref.shape[0] // 2
    other_refs, outs = refs[:-2], refs[-2:]
    for side in range(2):
        total = jnp.dot(int_ref[pl.ds(side * rows, rows), :], amp_ref[:, cols], preferred_element_type=jnp.float32)
        if other_refs:
            total = (total + other_refs[side][...]).astype(jnp.bfloat16)
        outs[side][...] = total


def multiply(r, ints, amps, *other):
    rows, depth, width = ints.shape[0] // 2, ints.shape[1], amps.shape[1] // RCHUNKS
    vmem_spec = pl.BlockSpec(memory_space=VMEM)

    def kernel(*refs):
        multiply_kernel(slice(r * width, (r + 1) * width), *refs)

    return pl.pallas_call(
        kernel,
        in_specs=[vmem_spec] * (2 + len(other)),
        out_specs=[vmem_spec] * 2,
        out_shape=[jax.ShapeDtypeStruct((rows, width), jnp.bfloat16 if other else jnp.float32)] * 2,
        cost_estimate=pl.CostEstimate(
            flops=4 * rows * depth * width, bytes_accessed=(2 * rows + width) * depth * 2 + 8 * rows * width, transcendentals=0
        ),
        compiler_params=pltpu.CompilerParams(vmem_limit_bytes=12 * MIB),
        name="multiply_own" if other else "multiply_other",
    )(ints, amps, *other)


def body(amplitudes, integrals, amp_mask, int_mask):
    pair, z, conv = (lax.axis_index(name) for name in AXES)
    x_hi, core = conv // 2, conv % 2
    x_lo, y = pair // NY, pair % NY
    place = jnp.stack([pair, z, x_hi, x_hi * 2 + x_lo, y, core]).astype(jnp.int32)

    keep, give = mask_amplitudes(place, amp_mask, amplitudes.T)
    int_t, keep, give = lax.optimization_barrier((integrals.T, keep, give))
    first, second = mask_integrals(place, int_mask, int_t)
    chains = [ring_of_eight(keep), ring_of_eight(send(give, X_ACROSS))]
    ints = plane(first, (X_FIRST, X_OTHER), (Y_FIRST, Y_OTHER)) + plane(second, (Y_FIRST, Y_OTHER), (X_FIRST, X_OTHER))
    amps = order_amplitudes(place, chains)
    other_ints, own_ints = order_integrals(place, ints)

    kept, received = [], []
    for r in range(RCHUNKS):
        partials = [send(partial, CORE) for partial in multiply(r, other_ints, amps)]
        theirs, mine = multiply(r, own_ints, amps, *partials)
        kept.append(mine)
        received.append(send(theirs, X_ACROSS))
    low = [jnp.where(x_hi == 0, k, g) for k, g in zip(kept, received)]
    high = [jnp.where(x_hi == 0, g, k) for k, g in zip(kept, received)]
    return jnp.concatenate(low + high, axis=1)


def solution(mesh):
    placed = (
        P("pair", ("conv", "outv")),
        P("conv", ("outv", "pair")),
        P("pair", "conv"),
        P("conv", "outv"),
    )
    return jax.shard_map(
        body, mesh=mesh, in_specs=placed, out_specs=P(("outv", "conv"), "pair"), check_vma=False
    )
```

```python
import jax
import jax.numpy as jnp
from jax import lax
from jax.experimental import pallas as pl
from jax.experimental.pallas import tpu as pltpu
from jax.sharding import PartitionSpec as P

TW = 96
AXES = ("pair", "outv", "conv")
NX, NY, NZ = 4, 4, 8
RCHUNKS = 2
DEPTH_X = 768
MIB = 1024 * 1024
VMEM = pltpu.MemorySpace.VMEM
SMEM = pltpu.MemorySpace.SMEM


def index_of(x, y, z, c):
    x, y, z = x % NX, y % NY, z % NZ
    return ((x % 2) * NY + y) * (NZ * 4) + z * 4 + (x // 2) * 2 + c


def moves(target):
    return [
        (index_of(x, y, z, c), index_of(*target(x, y, z, c)))
        for x in range(NX)
        for y in range(NY)
        for z in range(NZ)
        for c in range(2)
    ]


def sign(i, c):
    return 1 - 2 * ((i + c) % 2)


X_FIRST = moves(lambda x, y, z, c: (x + sign(x, c), y, z, c))
X_OTHER = moves(lambda x, y, z, c: (x - sign(x, c), y, z, c))
Y_FIRST = moves(lambda x, y, z, c: (x, y + sign(y, c), z, c))
Y_OTHER = moves(lambda x, y, z, c: (x, y - sign(y, c), z, c))
Z_FIRST = moves(lambda x, y, z, c: (x, y, z + sign(z, c), c))
Z_OTHER = moves(lambda x, y, z, c: (x, y, z - sign(z, c), c))
X_ACROSS = moves(lambda x, y, z, c: (x + 2, y, z, c))
CORE = moves(lambda x, y, z, c: (x, y, z, 1 - c))
RING4 = (0, 1, -1, -2)
RING8 = (0, 1, -1, -2, 2, 3, -3, -4)


def send(array, plan):
    return lax.ppermute(array, AXES, plan)


def mask_integrals_kernel(place, mask_ref, int_ref, first_ref, second_ref):
    width = int_ref.shape[1]
    half = first_ref.shape[1]
    tile = lax.broadcasted_iota(jnp.int32, (8, width), 1) // TW
    for j in range(int_ref.shape[0] // TW):
        column = place[0] * (int_ref.shape[0] // TW) + j
        row = jnp.zeros((8, width), jnp.float32)
        for k in range(width // TW):
            row = jnp.where(tile == k, mask_ref[k, column].astype(jnp.float32), row)
        row = row[0:1, :].astype(jnp.bfloat16)
        rows = pl.ds(j * TW, TW)
        first_ref[rows, :] = int_ref[rows, :half] * row[:, :half]
        second_ref[rows, :] = int_ref[rows, half:] * row[:, half:]


def mask_integrals(place, int_mask, int_t):
    rows, width = int_t.shape
    shapes = [jax.ShapeDtypeStruct((rows, depth), jnp.bfloat16) for depth in (DEPTH_X, width - DEPTH_X)]
    return pl.pallas_call(
        mask_integrals_kernel,
        in_specs=[pl.BlockSpec(memory_space=SMEM), pl.BlockSpec(memory_space=SMEM), pl.BlockSpec(memory_space=VMEM)],
        out_specs=[pl.BlockSpec(memory_space=VMEM)] * 2,
        out_shape=shapes,
        compiler_params=pltpu.CompilerParams(vmem_limit_bytes=8 * MIB),
        name="mask_integrals",
    )(place, int_mask, int_t)


def mask_amplitudes_kernel(place, mask_ref, amp_ref, keep_ref, give_ref):
    width = keep_ref.shape[1]
    for j in range(amp_ref.shape[0] // TW):
        value = mask_ref[0, place[1] * (amp_ref.shape[0] // TW) + j].astype(jnp.float32)
        rows = pl.ds(j * TW, TW)
        row = jnp.full((1, width), value, jnp.float32).astype(jnp.bfloat16)
        for out_ref, side in ((give_ref, 1 - place[2]), (keep_ref, place[2])):
            out_ref[rows, :] = amp_ref[rows, pl.ds(pl.multiple_of(side * width, 128), width)] * row


def mask_amplitudes(place, amp_mask, amp_t):
    rows, width = amp_t.shape
    shape = jax.ShapeDtypeStruct((rows, width // 2), jnp.bfloat16)
    return pl.pallas_call(
        mask_amplitudes_kernel,
        in_specs=[pl.BlockSpec(memory_space=SMEM), pl.BlockSpec(memory_space=SMEM), pl.BlockSpec(memory_space=VMEM)],
        out_specs=[pl.BlockSpec(memory_space=VMEM)] * 2,
        out_shape=[shape] * 2,
        compiler_params=pltpu.CompilerParams(vmem_limit_bytes=8 * MIB),
        name="mask_amplitudes",
    )(place, amp_mask, amp_t)


def ring_of_eight(own):
    near = jnp.stack([own, send(own, Z_FIRST)])
    second = send(near, Z_OTHER)
    third = send(second, Z_FIRST)
    fourth = send(third, Z_OTHER)
    return [near, second, third, fourth]


def plane(own, first_axis, second_axis):
    near = jnp.stack([own, send(own, first_axis[0])])
    far = send(near, first_axis[1])
    pieces = []
    for group in (near, far):
        both = jnp.concatenate([group, send(group, second_axis[0])])
        pieces += [both, send(both, second_axis[1])]
    return pieces


def order_amplitudes_kernel(origins, place, *refs):
    pieces = refs[: len(origins)]
    out_ref, sems = refs[-2:]
    z, x_hi, c = place[1], place[2], place[5]
    rows = pieces[0].shape[1]
    sz = 1 - 2 * ((z + c) % 2)
    copies = []
    for (chain, step), piece in zip(origins, pieces):
        hi = x_hi if chain == 0 else 1 - x_hi
        for e in range(2):
            z_from = (z + sz * RING8[2 * step + e] + NZ) % NZ
            row = pl.multiple_of((hi * NZ + z_from) * rows, rows)
            for col in range(0, piece.shape[2], 256):
                copies.append(
                    pltpu.make_async_copy(
                        piece.at[e, :, pl.ds(col, 256)],
                        out_ref.at[pl.ds(row, rows), pl.ds(col, 256)],
                        sems.at[len(copies)],
                    )
                )
    for copy in copies:
        copy.start()
    for copy in copies:
        copy.wait()


def order_amplitudes(place, chains):
    _, rows, width = chains[0][0].shape
    any_spec, vmem_spec = pl.BlockSpec(memory_space=pl.ANY), pl.BlockSpec(memory_space=VMEM)
    held = []
    for origins in (((0, 0), (1, 0), (0, 1), (1, 1), (0, 2), (1, 2)), ((0, 3),), ((1, 3),)):
        pieces = [chains[chain][step] for chain, step in origins]

        def kernel(*refs, origins=origins):
            order_amplitudes_kernel(origins, *refs)

        held = [
            pl.pallas_call(
                kernel,
                in_specs=[pl.BlockSpec(memory_space=SMEM)] + [any_spec] * len(pieces) + [vmem_spec] * len(held),
                out_specs=vmem_spec,
                out_shape=pltpu.VMEM((16 * rows, width), jnp.bfloat16),
                scratch_shapes=[pltpu.SemaphoreType.DMA((2 * len(pieces) * width // 256,))],
                input_output_aliases={1 + len(pieces): 0} if held else {},
                cost_estimate=pl.CostEstimate(flops=0, bytes_accessed=8 * len(pieces) * rows * width, transcendentals=0),
                compiler_params=pltpu.CompilerParams(vmem_limit_bytes=MIB),
                name="order_amplitudes",
            )(place, *pieces, *held)
        ]
    return held[0]


def order_integrals_kernel(got, place, *refs):
    pieces = refs[:4]
    outs, sems = refs[-3:-1], refs[-1]
    x, y, c, x_hi = place[3], place[4], place[5], place[2]
    sx, sy = 1 - 2 * ((x + c) % 2), 1 - 2 * ((y + c) % 2)
    rows, depths = pieces[0].shape[1], (pieces[0].shape[2], pieces[2].shape[2])
    copies = []
    for half in range(2):
        for group in range(2):
            for step in range(2):
                for e in range(2):
                    near, far = RING4[2 * group + e], RING4[2 * got + step]
                    dx, dy = (near, far) if half == 0 else (far, near)
                    x_from, y_from = (x + sx * dx + NX) % NX, (y + sy * dy + NY) % NY
                    side = (x_from % 2 + x_hi + 1) % 2
                    row = pl.multiple_of((side * 2 + y_from % 2) * rows, rows)
                    col = pl.multiple_of((x_from // 2) * sum(depths) + half * depths[0], 128)
                    for own in range(2):
                        copy = pltpu.make_async_copy(
                            pieces[half * 2 + group].at[step * 2 + e],
                            outs[own].at[pl.ds(row, rows), pl.ds(col, depths[half])],
                            sems.at[len(copies)],
                        )
                        copies.append((y_from // 2 == (c if own else 1 - c), copy))
    for here, copy in copies:
        pl.when(here)(copy.start)
    for here, copy in copies:
        pl.when(here)(copy.wait)


def order_integrals(place, ints):
    any_spec, vmem_spec = pl.BlockSpec(memory_space=pl.ANY), pl.BlockSpec(memory_space=VMEM)
    out = pltpu.VMEM((768, 3072), jnp.bfloat16)
    held = []
    for got in range(2):
        args = [place, *ints[got::2], *held]

        def kernel(*refs, got=got):
            order_integrals_kernel(got, *refs)

        held = pl.pallas_call(
            kernel,
            in_specs=[pl.BlockSpec(memory_space=SMEM)] + [any_spec] * 4 + [vmem_spec] * len(held),
            out_specs=[vmem_spec] * 2,
            out_shape=[out] * 2,
            scratch_shapes=[pltpu.SemaphoreType.DMA((32,))],
            input_output_aliases={5: 0, 6: 1} if held else {},
            cost_estimate=pl.CostEstimate(flops=0, bytes_accessed=2 * 768 * 3072 * 2, transcendentals=0),
            compiler_params=pltpu.CompilerParams(vmem_limit_bytes=MIB),
            name="order_integrals",
        )(*args)
    return held


def multiply_kernel(cols, int_ref, amp_ref, *refs):
    rows = int_ref.shape[0] // 2
    for side in range(2):
        src = pl.ds(side * rows, rows)
        total = jnp.dot(int_ref[src, :], amp_ref[:, cols], preferred_element_type=jnp.float32)
        if len(refs) == 3:
            refs[1 + side][...] = (total + refs[0][src, :]).astype(jnp.bfloat16)
        else:
            refs[0][src, :] = total


def multiply(r, ints, amps, *other):
    rows, depth, width = ints.shape[0] // 2, ints.shape[1], amps.shape[1] // RCHUNKS
    vmem_spec = pl.BlockSpec(memory_space=VMEM)
    if other:
        shapes = [jax.ShapeDtypeStruct((rows, width), jnp.bfloat16)] * 2
    else:
        shapes = [jax.ShapeDtypeStruct((2 * rows, width), jnp.float32)]

    def kernel(*refs):
        multiply_kernel(slice(r * width, (r + 1) * width), *refs)

    return pl.pallas_call(
        kernel,
        in_specs=[vmem_spec] * (2 + len(other)),
        out_specs=[vmem_spec] * len(shapes),
        out_shape=shapes,
        cost_estimate=pl.CostEstimate(
            flops=4 * rows * depth * width, bytes_accessed=(2 * rows + width) * depth * 2 + 8 * rows * width, transcendentals=0
        ),
        compiler_params=pltpu.CompilerParams(vmem_limit_bytes=12 * MIB),
        name="multiply_own" if other else "multiply_other",
    )(ints, amps, *other)


def body(amplitudes, integrals, amp_mask, int_mask):
    pair, z, conv = (lax.axis_index(name) for name in AXES)
    x_hi, core = conv // 2, conv % 2
    x_lo, y = pair // NY, pair % NY
    place = jnp.stack([pair, z, x_hi, x_hi * 2 + x_lo, y, core]).astype(jnp.int32)

    keep, give = mask_amplitudes(place, amp_mask, amplitudes.T)
    int_t, keep, give = lax.optimization_barrier((integrals.T, keep, give))
    first, second = mask_integrals(place, int_mask, int_t)
    chains = [ring_of_eight(keep), ring_of_eight(send(give, X_ACROSS))]
    ints = plane(first, (X_FIRST, X_OTHER), (Y_FIRST, Y_OTHER)) + plane(second, (Y_FIRST, Y_OTHER), (X_FIRST, X_OTHER))
    amps = order_amplitudes(place, chains)
    other_ints, own_ints = order_integrals(place, ints)

    kept, received = [], []
    for r in range(RCHUNKS):
        (partial,) = multiply(r, other_ints, amps)
        theirs, mine = multiply(r, own_ints, amps, send(partial, CORE))
        kept.append(mine)
        received.append(send(theirs, X_ACROSS))
    low = [jnp.where(x_hi == 0, k, g) for k, g in zip(kept, received)]
    high = [jnp.where(x_hi == 0, g, k) for k, g in zip(kept, received)]
    return jnp.concatenate(low + high, axis=1)


def solution(mesh):
    placed = (
        P("pair", ("conv", "outv")),
        P("conv", ("outv", "pair")),
        P("pair", "conv"),
        P("conv", "outv"),
    )
    return jax.shard_map(
        body, mesh=mesh, in_specs=placed, out_specs=P(("outv", "conv"), "pair"), check_vma=False
    )
```

```python
import jax
import jax.numpy as jnp
from jax import lax
from jax.experimental import pallas as pl
from jax.experimental.pallas import tpu as pltpu
from jax.sharding import PartitionSpec as P

TW = 96
AXES = ("pair", "outv", "conv")
NX, NY, NZ = 4, 4, 8
RCHUNKS = 2
DEPTH_X = 768
MIB = 1024 * 1024
VMEM = pltpu.MemorySpace.VMEM
SMEM = pltpu.MemorySpace.SMEM


def index_of(x, y, z, c):
    x, y, z = x % NX, y % NY, z % NZ
    return ((x % 2) * NY + y) * (NZ * 4) + z * 4 + (x // 2) * 2 + c


def moves(target):
    return [
        (index_of(x, y, z, c), index_of(*target(x, y, z, c)))
        for x in range(NX)
        for y in range(NY)
        for z in range(NZ)
        for c in range(2)
    ]


def sign(i, c):
    return 1 - 2 * ((i + c) % 2)


X_FIRST = moves(lambda x, y, z, c: (x + sign(x, c), y, z, c))
X_OTHER = moves(lambda x, y, z, c: (x - sign(x, c), y, z, c))
Y_FIRST = moves(lambda x, y, z, c: (x, y + sign(y, c), z, c))
Y_OTHER = moves(lambda x, y, z, c: (x, y - sign(y, c), z, c))
Z_FIRST = moves(lambda x, y, z, c: (x, y, z + sign(z, c), c))
Z_OTHER = moves(lambda x, y, z, c: (x, y, z - sign(z, c), c))
X_ACROSS = moves(lambda x, y, z, c: (x + 2, y, z, c))
CORE = moves(lambda x, y, z, c: (x, y, z, 1 - c))
RING4 = (0, 1, -1, -2)
RING8 = (0, 1, -1, -2, 2, 3, -3, -4)


def send(array, plan):
    return lax.ppermute(array, AXES, plan)


def mask_integrals_kernel(place, mask_ref, int_ref, first_ref, second_ref):
    width = int_ref.shape[1]
    half = first_ref.shape[1]
    tile = lax.broadcasted_iota(jnp.int32, (8, width), 1) // TW
    for j in range(int_ref.shape[0] // TW):
        column = place[0] * (int_ref.shape[0] // TW) + j
        row = jnp.zeros((8, width), jnp.float32)
        for k in range(width // TW):
            row = jnp.where(tile == k, mask_ref[k, column].astype(jnp.float32), row)
        row = row[0:1, :].astype(jnp.bfloat16)
        rows = pl.ds(j * TW, TW)
        first_ref[rows, :] = int_ref[rows, :half] * row[:, :half]
        second_ref[rows, :] = int_ref[rows, half:] * row[:, half:]


def mask_integrals(place, int_mask, int_t):
    rows, width = int_t.shape
    shapes = [jax.ShapeDtypeStruct((rows, depth), jnp.bfloat16) for depth in (DEPTH_X, width - DEPTH_X)]
    return pl.pallas_call(
        mask_integrals_kernel,
        in_specs=[pl.BlockSpec(memory_space=SMEM), pl.BlockSpec(memory_space=SMEM), pl.BlockSpec(memory_space=VMEM)],
        out_specs=[pl.BlockSpec(memory_space=VMEM)] * 2,
        out_shape=shapes,
        compiler_params=pltpu.CompilerParams(vmem_limit_bytes=8 * MIB),
        name="mask_integrals",
    )(place, int_mask, int_t)


def mask_amplitudes_kernel(place, mask_ref, amp_ref, keep_ref, give_ref):
    width = keep_ref.shape[1]
    for j in range(amp_ref.shape[0] // TW):
        value = mask_ref[0, place[1] * (amp_ref.shape[0] // TW) + j].astype(jnp.float32)
        rows = pl.ds(j * TW, TW)
        row = jnp.full((1, width), value, jnp.float32).astype(jnp.bfloat16)
        for out_ref, side in ((give_ref, 1 - place[2]), (keep_ref, place[2])):
            out_ref[rows, :] = amp_ref[rows, pl.ds(pl.multiple_of(side * width, 128), width)] * row


def mask_amplitudes(place, amp_mask, amp_t):
    rows, width = amp_t.shape
    shape = jax.ShapeDtypeStruct((rows, width // 2), jnp.bfloat16)
    return pl.pallas_call(
        mask_amplitudes_kernel,
        in_specs=[pl.BlockSpec(memory_space=SMEM), pl.BlockSpec(memory_space=SMEM), pl.BlockSpec(memory_space=VMEM)],
        out_specs=[pl.BlockSpec(memory_space=VMEM)] * 2,
        out_shape=[shape] * 2,
        compiler_params=pltpu.CompilerParams(vmem_limit_bytes=8 * MIB),
        name="mask_amplitudes",
    )(place, amp_mask, amp_t)


def ring_of_eight(own):
    near = jnp.stack([own, send(own, Z_FIRST)])
    second = send(near, Z_OTHER)
    third = send(second, Z_FIRST)
    fourth = send(third, Z_OTHER)
    return [near, second, third, fourth]


def plane(own, first_axis, second_axis):
    near = jnp.stack([own, send(own, first_axis[0])])
    far = send(near, first_axis[1])
    pieces = []
    for group in (near, far):
        both = jnp.concatenate([group, send(group, second_axis[0])])
        pieces += [both, send(both, second_axis[1])]
    return pieces


def order_amplitudes_kernel(origins, place, *refs):
    pieces = refs[: len(origins)]
    out_ref, sems = refs[-2:]
    z, x_hi, c = place[1], place[2], place[5]
    rows = pieces[0].shape[1]
    sz = 1 - 2 * ((z + c) % 2)
    copies = []
    for (chain, step), piece in zip(origins, pieces):
        hi = x_hi if chain == 0 else 1 - x_hi
        for e in range(2):
            z_from = (z + sz * RING8[2 * step + e] + NZ) % NZ
            row = pl.multiple_of((hi * NZ + z_from) * rows, rows)
            for col in range(0, piece.shape[2], 256):
                copies.append(
                    pltpu.make_async_copy(
                        piece.at[e, :, pl.ds(col, 256)],
                        out_ref.at[pl.ds(row, rows), pl.ds(col, 256)],
                        sems.at[len(copies)],
                    )
                )
    for copy in copies:
        copy.start()
    for copy in copies:
        copy.wait()


def order_amplitudes(place, chains):
    _, rows, width = chains[0][0].shape
    any_spec, vmem_spec = pl.BlockSpec(memory_space=pl.ANY), pl.BlockSpec(memory_space=VMEM)
    held = []
    for origins in (((0, 0), (1, 0), (0, 1), (1, 1), (0, 2), (1, 2)), ((0, 3),), ((1, 3),)):
        pieces = [chains[chain][step] for chain, step in origins]

        def kernel(*refs, origins=origins):
            order_amplitudes_kernel(origins, *refs)

        held = [
            pl.pallas_call(
                kernel,
                in_specs=[pl.BlockSpec(memory_space=SMEM)] + [any_spec] * len(pieces) + [vmem_spec] * len(held),
                out_specs=vmem_spec,
                out_shape=pltpu.VMEM((16 * rows, width), jnp.bfloat16),
                scratch_shapes=[pltpu.SemaphoreType.DMA((2 * len(pieces) * width // 256,))],
                input_output_aliases={1 + len(pieces): 0} if held else {},
                cost_estimate=pl.CostEstimate(flops=0, bytes_accessed=8 * len(pieces) * rows * width, transcendentals=0),
                compiler_params=pltpu.CompilerParams(vmem_limit_bytes=MIB),
                name="order_amplitudes",
            )(place, *pieces, *held)
        ]
    return held[0]


def order_integrals_kernel(got, place, *refs):
    pieces = refs[:4]
    outs, sems = refs[-3:-1], refs[-1]
    x, y, c, x_hi = place[3], place[4], place[5], place[2]
    sx, sy = 1 - 2 * ((x + c) % 2), 1 - 2 * ((y + c) % 2)
    rows, depths = pieces[0].shape[1], (pieces[0].shape[2], pieces[2].shape[2])
    copies = []
    for half in range(2):
        for group in range(2):
            for step in range(2):
                for e in range(2):
                    near, far = RING4[2 * group + e], RING4[2 * got + step]
                    dx, dy = (near, far) if half == 0 else (far, near)
                    x_from, y_from = (x + sx * dx + NX) % NX, (y + sy * dy + NY) % NY
                    side = (x_from % 2 + x_hi + 1) % 2
                    row = pl.multiple_of((side * 2 + y_from % 2) * rows, rows)
                    col = pl.multiple_of((x_from // 2) * sum(depths) + half * depths[0], 128)
                    for own in range(2):
                        copy = pltpu.make_async_copy(
                            pieces[half * 2 + group].at[step * 2 + e],
                            outs[own].at[pl.ds(row, rows), pl.ds(col, depths[half])],
                            sems.at[len(copies)],
                        )
                        copies.append((y_from // 2 == (c if own else 1 - c), copy))
    for here, copy in copies:
        pl.when(here)(copy.start)
    for here, copy in copies:
        pl.when(here)(copy.wait)


def order_integrals(place, ints):
    any_spec, vmem_spec = pl.BlockSpec(memory_space=pl.ANY), pl.BlockSpec(memory_space=VMEM)
    out = pltpu.VMEM((768, 3072), jnp.bfloat16)
    held = []
    for got in range(2):
        args = [place, *ints[got::2], *held]

        def kernel(*refs, got=got):
            order_integrals_kernel(got, *refs)

        held = pl.pallas_call(
            kernel,
            in_specs=[pl.BlockSpec(memory_space=SMEM)] + [any_spec] * 4 + [vmem_spec] * len(held),
            out_specs=[vmem_spec] * 2,
            out_shape=[out] * 2,
            scratch_shapes=[pltpu.SemaphoreType.DMA((32,))],
            input_output_aliases={5: 0, 6: 1} if held else {},
            cost_estimate=pl.CostEstimate(flops=0, bytes_accessed=2 * 768 * 3072 * 2, transcendentals=0),
            compiler_params=pltpu.CompilerParams(vmem_limit_bytes=MIB),
            name="order_integrals",
        )(*args)
    return held


def multiply_kernel(cols, int_ref, amp_ref, *refs):
    rows = int_ref.shape[0] // 2
    for side in range(2):
        src = pl.ds(side * rows, rows)
        total = jnp.dot(int_ref[src, :], amp_ref[:, cols], preferred_element_type=jnp.float32)
        if len(refs) == 3:
            refs[1 + side][...] = (total + refs[0][src, :]).astype(jnp.bfloat16)
        else:
            refs[0][src, :] = total


def multiply(r, ints, amps, *other):
    rows, depth, width = ints.shape[0] // 2, ints.shape[1], amps.shape[1] // RCHUNKS
    vmem_spec = pl.BlockSpec(memory_space=VMEM)
    if other:
        shapes = [jax.ShapeDtypeStruct((rows, width), jnp.bfloat16)] * 2
    else:
        shapes = [jax.ShapeDtypeStruct((2 * rows, width), jnp.float32)]

    def kernel(*refs):
        multiply_kernel(slice(r * width, (r + 1) * width), *refs)

    return pl.pallas_call(
        kernel,
        in_specs=[vmem_spec] * (2 + len(other)),
        out_specs=[vmem_spec] * len(shapes),
        out_shape=shapes,
        cost_estimate=pl.CostEstimate(
            flops=4 * rows * depth * width, bytes_accessed=(2 * rows + width) * depth * 2 + 8 * rows * width, transcendentals=0
        ),
        compiler_params=pltpu.CompilerParams(vmem_limit_bytes=12 * MIB),
        name="multiply_own" if other else "multiply_other",
    )(ints, amps, *other)


def body(amplitudes, integrals, amp_mask, int_mask):
    pair, z, conv = (lax.axis_index(name) for name in AXES)
    x_hi, core = conv // 2, conv % 2
    x_lo, y = pair // NY, pair % NY
    place = jnp.stack([pair, z, x_hi, x_hi * 2 + x_lo, y, core]).astype(jnp.int32)

    keep, give = mask_amplitudes(place, amp_mask, amplitudes.T)
    first, second = mask_integrals(place, int_mask, integrals.T)
    chains = [ring_of_eight(keep), ring_of_eight(send(give, X_ACROSS))]
    ints = plane(first, (X_FIRST, X_OTHER), (Y_FIRST, Y_OTHER)) + plane(second, (Y_FIRST, Y_OTHER), (X_FIRST, X_OTHER))
    amps = order_amplitudes(place, chains)
    other_ints, own_ints = order_integrals(place, ints)

    kept, received = [], []
    for r in range(RCHUNKS):
        (partial,) = multiply(r, other_ints, amps)
        theirs, mine = multiply(r, own_ints, amps, send(partial, CORE))
        kept.append(mine)
        received.append(send(theirs, X_ACROSS))
    low = [jnp.where(x_hi == 0, k, g) for k, g in zip(kept, received)]
    high = [jnp.where(x_hi == 0, g, k) for k, g in zip(kept, received)]
    return jnp.concatenate(low + high, axis=1)


def solution(mesh):
    placed = (
        P("pair", ("conv", "outv")),
        P("conv", ("outv", "pair")),
        P("pair", "conv"),
        P("conv", "outv"),
    )
    return jax.shard_map(
        body, mesh=mesh, in_specs=placed, out_specs=P(("outv", "conv"), "pair"), check_vma=False
    )
```
